32 devices in a mesh: seq: 8 (over y, x, core), expert: 4 (over z).
Axes of the slice: x: 2, y: 2, z: 4, core: 2. Of those that a mesh axis runs over, the one named last changes fastest.
Arguments:
- x_in: bfloat16 [1024, 4096], P('seq', 'expert'), may hold values from -6 to 6
- z_in: bfloat16 [1024, 4096], P('seq', 'expert'), may hold values from -6 to 6
- dt_raw: float32 [1024, 4096], P('seq', 'expert'), may hold values from -4 to 4
- bc_in: float32 [2, 16, 1024], P(None, None, 'seq'), may hold values from -6 to 6
- a_log: float32 [16, 4096], P(None, 'expert'), may hold values from -2 to 1.5
- conv_weight: float32 [4, 4096], P(None, 'expert'), may hold values from -3 to 3
- conv_bias: float32 [4096], P('expert'), may hold values from -3 to 3
- skip_gain: float32 [4096], P('expert'), may hold values from 0.25 to 1.75
- dt_bias: float32 [4096], P('expert'), may hold values from -6 to -1
- out_weight: bfloat16 [4096, 2048], P('expert'), may hold values from -0.09375 to 0.09375
- resid: bfloat16 [1024, 2048], P(('seq', 'expert')), may hold values from -6 to 6
- w_gate: bfloat16 [4, 2048, 7168], P('expert', None, 'seq'), may hold values from -0.125 to 0.125
- w_up: bfloat16 [4, 2048, 7168], P('expert', None, 'seq'), may hold values from -0.125 to 0.125
- w_down: bfloat16 [4, 7168, 2048], P('expert', 'seq'), may hold values from -0.0625 to 0.0625
- route_ids: int32 [1024, 2], P(('seq', 'expert')), may hold values from 0 to 3, all different within a row; in each aligned block of 32 rows (0 to 31, 32 to 63, ...) at most 32 rows name the same one
- route_weight: float32 [1024, 2], P(('seq', 'expert')), may hold values from 0.2 to 0.8
- grad_mix: bfloat16 [1024, 2048], P('seq'), may hold values from -6 to 6
Outputs:
- layer_out: bfloat16 [1024, 2048], P(('seq', 'expert'))
- grad_x: float32 [1024, 4096], P('seq', 'expert')
- grad_z: float32 [1024, 4096], P('seq', 'expert')
- grad_dt: float32 [1024, 4096], P('seq', 'expert')
- grad_bc: float32 [2, 16, 1024], P(None, None, 'seq')
- grad_alog: float32 [16, 4096], P(None, 'expert')
- grad_conv: float32 [4, 4096], P(None, 'expert')
- grad_chan: float32 [3, 4096], P(None, 'expert')
The draws below stay inside these ranges and needn't reach their ends.
Inputs may be any that keep to these rules, and one draw needn't show every extreme that they name: `route_ids`: within the 32 rows of one device no expert is named by more than 32 rows; some expert is named by exactly 32. The two experts of a token differ.
All inputs are finite; a program needn't handle non-finite values.
Results may differ from the reference program's by a relative error of at most 0.028.
Values may be sent and summed in bfloat16 or wider, within the bound.
A program may use at most 128 MiB of HBM per device.

```python
import math
import jax
import jax.numpy as jnp
import numpy as np
from jax import lax

DM = 2048
CH = 4096
NS = 16
KW = 4
HID = 7168
EXPERTS = 4
TOKENS = 1024
ROWS = 32
CAP = 32
N_SEQ = 8


def shard_levels(key, dims, shards, low, largest):
    def one(dim, shards_of):
        heights = jax.random.uniform(jax.random.fold_in(jax.random.fold_in(key, 6), dim), (shards_of,), jnp.float32, low / len(shards), largest / len(shards))
        return jnp.repeat(jnp.exp(heights), dims[dim] // shards_of).reshape((-1,) + (1,) * (len(dims) - dim - 1))

    level = one(*shards[0])
    for cut in shards[1:]:
        level = level * one(*cut)
    return level


def deal_out(own_key, own, number, rows, count, top, bound, lean):
    order = jax.random.permutation(own_key, count)
    heavy_load, common = portions_of(count, rows * top, bound, lean, True), portions_of(count, rows * top, bound, lean, False)
    places = jnp.arange(count)

    def named(sizes, turn):
        used = int((sizes > 0).sum())
        fixed = max(1, used // 4)
        passed = fixed + (places - fixed + turn * (used - fixed)) % max(1, count - fixed)
        return jnp.zeros((count,), jnp.int32).at[order[jnp.where(places < fixed, places, passed)]].set(jnp.asarray(sizes, jnp.int32))

    sizes = jnp.where(number % 4 == 0, named(heavy_load, number // 4), named(common, number - number // 4 - 1))
    mixed = jax.random.permutation(jax.random.fold_in(own, 3), count)
    source_of, taker = mixed[0:count // 2 * 2:2], mixed[1:count // 2 * 2:2]
    room = jnp.minimum(sizes[source_of] - 1, bound - sizes[taker]) // 2
    room = jnp.where((source_of == order[0]) | (taker == order[0]) | (sizes[taker] == 0), 0, jnp.maximum(room, 0))
    passed = jax.random.randint(jax.random.fold_in(own, 4), (count // 2,), 0, 1 << 20) % (room + 1)
    sizes = sizes.at[source_of].add(-passed).at[taker].add(passed)
    members = jnp.searchsorted(jnp.cumsum(sizes), jnp.arange(rows * top), side="right").astype(jnp.int32)
    listing = members.reshape(top, rows).T
    listing = listing[jax.random.permutation(jax.random.fold_in(own, 1), rows)]
    turn = jax.random.randint(jax.random.fold_in(own, 2), (rows, 1), 0, top)
    return jnp.take_along_axis(listing, (jnp.arange(top)[None, :] + turn) % top, axis=1)


def portions_of(number_of, total, reach, lean, full):
    portions = [(1 << 20) // math.isqrt(grade ** lean) + 1 for grade in range(1, number_of + 1)]
    largest = reach if full else min(reach, max(-(-total // number_of), total * portions[0] // sum(portions)))
    least = 1 if total - largest >= number_of - 1 else 0
    holding, rest = [largest] + [least] * (number_of - 1), total - largest - least * (number_of - 1)
    while rest > 0:
        movable = [i for i in range(1, number_of) if holding[i] < largest] or [i for i in range(1, number_of) if holding[i] < reach]
        pool, left = sum([portions[i] for i in movable]), rest
        for i in movable:
            addition = min(reach - holding[i], max(1, left * portions[i] // pool), rest)
            holding[i] = holding[i] + addition
            rest = rest - addition
    return np.array(holding)


def centred(own_key, shape, spread, reach, split=(), kind=jnp.bfloat16):
    factor_of = shard_levels(own_key, shape, split, -0.22, 0.18) if split else 1.0
    drawn = jax.random.normal(own_key, shape, jnp.float32) * spread * factor_of
    return jnp.minimum(jnp.maximum(drawn, -reach), reach).astype(kind)


def setup_inputs(seed: int = 0) -> dict:
    keys = jax.random.split(jax.random.key(seed), 18)
    x_in = centred(keys[0], (TOKENS, CH), 1.0, 6.0, ((0, 8), (1, 4)))
    z_in = centred(keys[1], (TOKENS, CH), 1.0, 6.0, ((0, 8), (1, 4)))
    dt_raw = centred(keys[2], (TOKENS, CH), 1.0, 4.0, ((0, 8), (1, 4)), jnp.float32)
    bc_in = centred(keys[3], (2, NS, TOKENS), 1.0, 6.0, ((2, 8),), jnp.float32)
    a_log = jnp.clip(-2.0 + 3.5 * jax.random.uniform(keys[4], (NS, CH), jnp.float32) ** shard_levels(keys[4], (NS, CH), ((1, 4),), -0.2, 0.2), -2.0, 1.5)
    conv_weight = centred(keys[5], (KW, CH), KW ** -0.5, 3.0, ((1, 4),), jnp.float32)
    conv_bias = centred(keys[6], (CH,), 0.5, 3.0, ((0, 4),), jnp.float32)
    skip_gain = jnp.clip(1.0 + 0.15 * jax.random.normal(keys[7], (CH,), jnp.float32), 0.25, 1.75)
    dt_bias = jnp.clip(-6.0 + 5.0 * jax.random.uniform(keys[8], (CH,), jnp.float32) ** shard_levels(keys[8], (CH,), ((0, 4),), -0.2, 0.2), -6.0, -1.0)
    out_weight = centred(keys[9], (CH, DM), CH ** -0.5, 0.09375, ((0, 4),))
    resid = centred(keys[10], (TOKENS, DM), 1.0, 6.0, ((0, 32),))
    w_gate = centred(keys[11], (EXPERTS, DM, HID), DM ** -0.5, 0.125, ((0, 4), (2, 8)))
    w_up = centred(keys[12], (EXPERTS, DM, HID), DM ** -0.5, 0.125, ((0, 4), (2, 8)))
    w_down = centred(keys[13], (EXPERTS, HID, DM), HID ** -0.5, 0.0625, ((0, 4), (1, 8)))
    route_ids_keys = jax.random.split(jax.random.fold_in(keys[14], 1), TOKENS // ROWS)
    route_ids_turns = jax.random.permutation(jax.random.fold_in(keys[14], 3), TOKENS // ROWS)
    route_ids = jax.vmap(lambda own, number: deal_out(jax.random.fold_in(keys[14], 2), own, number, ROWS, EXPERTS, 2, CAP, 2))(route_ids_keys, route_ids_turns).reshape((TOKENS, 2))
    route_weight = jnp.clip(0.2 + 0.6 * jax.random.uniform(keys[15], (TOKENS, 2), jnp.float32) ** shard_levels(keys[15], (TOKENS, 2), ((0, 32),), -0.2, 0.2), 0.2, 0.8)
    grad_mix = centred(keys[16], (TOKENS, DM), 1.0, 6.0, ((0, 8),))
    return dict(x_in=x_in, z_in=z_in, dt_raw=dt_raw, bc_in=bc_in, a_log=a_log, conv_weight=conv_weight, conv_bias=conv_bias, skip_gain=skip_gain, dt_bias=dt_bias, out_weight=out_weight, resid=resid, w_gate=w_gate, w_up=w_up, w_down=w_down, route_ids=route_ids, route_weight=route_weight, grad_mix=grad_mix)


def pair_combine(earlier, later):
    return (earlier[0] * later[0], later[0] * earlier[1] + later[1])

def mixer_core(x_val, dt_val, bc_val, a_val, conv_val, bias_val, skip_val, dtb_val):
    length = x_val.shape[0]
    padded = jnp.concatenate([jnp.zeros((KW - 1, x_val.shape[1]), jnp.float32), x_val], axis=0)
    pre = bias_val[None, :] + conv_val[0][None, :] * padded[0:length]
    for tap in range(1, KW):
        pre = pre + conv_val[tap][None, :] * padded[tap:tap + length]
    conv_out = jax.nn.silu(pre)
    step = jax.nn.softplus(dt_val + dtb_val[None, :])
    rate = -jnp.exp(a_val)
    decay = jnp.exp(step[:, None, :] * rate[None])
    drive = step[:, None, :] * bc_val[0].T[:, :, None] * conv_out[:, None, :]
    states = lax.associative_scan(pair_combine, (decay, drive), axis=0)[1]
    return lax.optimization_barrier(jnp.sum(bc_val[1].T[:, :, None] * states, axis=1)) + skip_val[None, :] * conv_out

def reference(x_in, z_in, dt_raw, bc_in, a_log, conv_weight, conv_bias, skip_gain, dt_bias, out_weight, resid, w_gate, w_up, w_down, route_ids, route_weight, grad_mix):
    width = math.gcd(CH, 256)
    nblk = CH // width

    def split_cols(arr):
        lead = arr.shape[:-1]
        return jnp.moveaxis(arr.reshape(lead + (nblk, width)), -2, 0)

    def join_cols(arr):
        moved = jnp.moveaxis(arr, 0, -2)
        return moved.reshape(moved.shape[:-2] + (CH,))
    back_mix = lax.dot_general(grad_mix, out_weight, (((1,), (1,)), ((), ())), preferred_element_type=jnp.float32)

    def block_work(pieces):
        xb, zb, db, ab, cwb, cbb, sgb, dbb, gb = pieces
        yb, pull = jax.vjp(mixer_core, xb, db, bc_in, ab, cwb, cbb, sgb, dbb)
        sig = jax.nn.sigmoid(zb)
        gated = yb * zb * sig
        grad_y = gb * zb * sig
        grad_zb = gb * yb * sig * (1.0 + zb * (1.0 - sig))
        return (gated, grad_zb) + tuple(pull(grad_y))
    results = lax.map(block_work, (split_cols(x_in.astype(jnp.float32)), split_cols(z_in.astype(jnp.float32)), split_cols(dt_raw), split_cols(a_log), split_cols(conv_weight), split_cols(conv_bias), split_cols(skip_gain), split_cols(dt_bias), split_cols(back_mix)))
    gated = join_cols(results[0]).astype(jnp.bfloat16)
    grad_z = join_cols(results[1])
    grad_x = join_cols(results[2])
    grad_dt = join_cols(results[3])
    grad_bc = lax.optimization_barrier(jnp.sum(results[4], axis=0))
    grad_alog = join_cols(results[5])
    grad_conv = join_cols(results[6])
    grad_chan = jnp.stack([join_cols(results[7]), join_cols(results[8]), join_cols(results[9])])
    mixed = jnp.dot(gated, out_weight, preferred_element_type=jnp.float32)
    hidden_in = (resid.astype(jnp.float32) + mixed).astype(jnp.bfloat16)
    nblocks = TOKENS // ROWS
    slot_count = nblocks * CAP
    flat_ids = route_ids.reshape(nblocks, ROWS * 2)
    onehot = (flat_ids[:, :, None] == jnp.arange(EXPERTS, dtype=jnp.int32)[None, None, :]).astype(jnp.int32)
    rank = lax.optimization_barrier(jnp.sum(jnp.cumsum(onehot, axis=1) * onehot, axis=2)) - 1
    target = flat_ids * slot_count + jnp.arange(nblocks, dtype=jnp.int32)[:, None] * CAP + rank
    target = target.reshape(-1).astype(jnp.int32)
    doubled = jnp.repeat(hidden_in, 2, axis=0)
    buffer = jnp.zeros((EXPERTS * slot_count, DM), jnp.bfloat16).at[target].set(doubled)
    buffer = buffer.reshape(EXPERTS, slot_count, DM)
    hid_dev = HID // N_SEQ

    def expert_work(pieces):
        rows_e, gate_w, up_w, down_w = pieces
        rows_f = rows_e.astype(jnp.float32)
        gate = jnp.dot(rows_f, gate_w.astype(jnp.float32), precision=lax.Precision.HIGHEST)
        upper = jnp.dot(rows_f, up_w.astype(jnp.float32), precision=lax.Precision.HIGHEST)
        hidden = (jax.nn.silu(gate) * upper).astype(jnp.bfloat16)
        hid_blocks = jnp.transpose(hidden.reshape(slot_count, N_SEQ, hid_dev), (1, 0, 2))
        down_blocks = down_w.reshape(N_SEQ, hid_dev, DM)

        def add_block(total, pair):
            part = jnp.dot(pair[0], pair[1], preferred_element_type=jnp.float32).astype(jnp.bfloat16)
            part = lax.optimization_barrier(part)
            return (total + part.astype(jnp.float32), None)
        total, _ = lax.scan(add_block, jnp.zeros((slot_count, DM), jnp.float32), (hid_blocks, down_blocks))
        return total.astype(jnp.bfloat16)
    outs = lax.map(expert_work, (buffer, w_gate, w_up, w_down))
    picked = outs.reshape(-1, DM)[target].astype(jnp.float32).reshape(TOKENS, 2, DM)
    moe = picked[:, 0] * route_weight[:, 0:1] + picked[:, 1] * route_weight[:, 1:2]
    layer_out = (hidden_in.astype(jnp.float32) + moe).astype(jnp.bfloat16)
    return (layer_out, grad_x, grad_z, grad_dt, grad_bc, grad_alog, grad_conv, grad_chan)
```

```python
import jax
import jax.numpy as jnp
from jax import lax
from jax.experimental import pallas as pl
from jax.experimental.pallas import tpu as pltpu
from jax.sharding import PartitionSpec as P

KW = 4
SUB = 8
LANES = 128


def shifted(x, axis, by):
    peers = lax.axis_size(axis)
    pairs = [(i, i + by) for i in range(peers) if 0 <= i + by < peers]
    return lax.ppermute(x, axis, pairs)


def wide(tile, width):
    return jnp.concatenate([tile] * (width // tile.shape[1]), axis=1)


def folded(value):
    total = value[:, :LANES]
    for at in range(LANES, value.shape[1], LANES):
        total = total + value[:, at : at + LANES]
    return total


def totals_kernel(step_ref, drive_ref, grad_ref, b_ref, c_ref, rate_ref, out_ref):
    rate = rate_ref[...]
    width = rate.shape[1]

    def advance(i, carry):
        state, passed, leaving = carry
        for j in range(SUB):
            decay = jnp.exp(step_ref[i, j : j + 1, :] * rate)
            state = decay * state + drive_ref[i, j : j + 1, :] * wide(b_ref[i, j], width)
            passed = passed * decay
            leaving = leaving + passed * (grad_ref[i, j : j + 1, :] * wide(c_ref[i, j], width))
        return (state, passed, leaving)

    zero = jnp.zeros_like(rate)
    state, passed, leaving = lax.fori_loop(
        0, step_ref.shape[0], advance, (zero, jnp.ones_like(rate), zero)
    )
    out_ref[0] = passed.astype(out_ref.dtype)
    out_ref[1] = state.astype(out_ref.dtype)
    out_ref[2] = leaving.astype(out_ref.dtype)


def forward_kernel(step_ref, drive_ref, b_ref, c_ref, rate_ref, start_ref, y_ref):
    rate = rate_ref[...]
    width = rate.shape[1]

    def advance(i, state):
        for j in range(SUB):
            decay = jnp.exp(step_ref[i, j : j + 1, :] * rate)
            state = decay * state + drive_ref[i, j : j + 1, :] * wide(b_ref[i, j], width)
            y_ref[i, j : j + 1, :] = jnp.sum(
                wide(c_ref[i, j], width) * state, axis=0, keepdims=True
            )
        return state

    lax.fori_loop(0, step_ref.shape[0], advance, start_ref[...])


def backward_kernel(
    step_ref,
    drive_ref,
    conv_ref,
    grad_ref,
    b_ref,
    c_ref,
    rate_ref,
    start_ref,
    arriving_ref,
    step_out_ref,
    conv_out_ref,
    b_out_ref,
    c_out_ref,
    alog_ref,
    states,
):
    rate = rate_ref[...]
    width = rate.shape[1]
    groups = step_ref.shape[0]

    @pl.when(pl.program_id(0) == 0)
    def _():
        b_out_ref[...] = jnp.zeros_like(b_out_ref)
        c_out_ref[...] = jnp.zeros_like(c_out_ref)

    states[0] = start_ref[...]

    def advance(i, state):
        for j in range(SUB):
            decay = jnp.exp(step_ref[i, j : j + 1, :] * rate)
            state = decay * state + drive_ref[i, j : j + 1, :] * wide(b_ref[i, j], width)
            states[i * SUB + j + 1] = state
        return state

    lax.fori_loop(0, groups, advance, start_ref[...])

    def retreat(k, carry):
        flow, alog_sum = carry
        i = groups - 1 - k
        for j in reversed(range(SUB)):
            at = i * SUB + j
            step_now = step_ref[i, j : j + 1, :]
            grad_now = grad_ref[i, j : j + 1, :]
            decay = jnp.exp(step_now * rate)
            adjoint = wide(c_ref[i, j], width) * grad_now + flow
            flow = decay * adjoint
            held = flow * states[at]
            alog_sum = alog_sum + step_now * held
            into_drive = jnp.sum(adjoint * wide(b_ref[i, j], width), axis=0, keepdims=True)
            step_out_ref[i, j : j + 1, :] = (
                jnp.sum(rate * held, axis=0, keepdims=True)
                + conv_ref[i, j : j + 1, :] * into_drive
            )
            conv_out_ref[i, j : j + 1, :] = step_now * into_drive
            b_out_ref[i, j] += folded(adjoint * drive_ref[i, j : j + 1, :])
            c_out_ref[i, j] += folded(grad_now * states[at + 1])
        return (flow, alog_sum)

    _, alog_sum = lax.fori_loop(0, groups, retreat, (arriving_ref[...], jnp.zeros_like(rate)))
    alog_ref[...] = alog_sum * rate


def sweeps(length, channels, states):
    block = min(512, channels)
    groups = length // SUB
    rows = pl.BlockSpec((groups, SUB, block), lambda k: (0, 0, k))
    spread = pl.BlockSpec((groups, SUB, states, LANES), lambda k: (0, 0, 0, 0))
    column = pl.BlockSpec((states, block), lambda k: (0, k))
    grid = (channels // block,)
    f32 = jnp.float32
    row_shape = jax.ShapeDtypeStruct((groups, SUB, channels), f32)
    spread_shape = jax.ShapeDtypeStruct((groups, SUB, states, LANES), f32)
    column_shape = jax.ShapeDtypeStruct((states, channels), f32)
    totals = pl.pallas_call(
        totals_kernel,
        grid=grid,
        in_specs=[rows, rows, rows, spread, spread, column],
        out_specs=pl.BlockSpec((3, states, block), lambda k: (0, 0, k)),
        out_shape=jax.ShapeDtypeStruct((3, states, channels), jnp.bfloat16),
        name="totals",
    )
    forward = pl.pallas_call(
        forward_kernel,
        grid=grid,
        in_specs=[rows, rows, spread, spread, column, column],
        out_specs=rows,
        out_shape=row_shape,
        name="forward",
    )
    backward = pl.pallas_call(
        backward_kernel,
        grid=grid,
        in_specs=[rows, rows, rows, rows, spread, spread, column, column, column],
        out_specs=[rows, rows, spread, spread, column],
        out_shape=[row_shape, row_shape, spread_shape, spread_shape, column_shape],
        scratch_shapes=[pltpu.VMEM((length + 1, states, block), f32)],
        name="backward",
    )
    return totals, forward, backward


def entering(everything):
    peers, here = everything.shape[0], lax.axis_index("seq")
    values = everything.astype(jnp.float32)
    start = jnp.zeros_like(values[0, 0])
    arriving = jnp.zeros_like(start)
    for k in range(peers):
        start = jnp.where(k < here, values[k, 0] * start + values[k, 1], start)
        back = peers - 1 - k
        arriving = jnp.where(back > here, values[back, 0] * arriving + values[back, 2], arriving)
    return start, arriving


def dense_experts(partial_value, resid, w_gate, w_up, w_down, route_ids, route_weight):
    rows = resid.shape[0]
    experts = lax.axis_size("expert")
    mine = lax.axis_index("expert")
    chosen = route_ids[:, :, None] == jnp.arange(experts, dtype=jnp.int32)[None, None, :]
    share = jnp.sum(jnp.where(chosen, route_weight[:, :, None], 0.0), axis=1)
    every_share = lax.all_gather(share, ("seq", "expert"), axis=0, tiled=True)
    is_mine = jnp.arange(experts, dtype=jnp.int32)[None, :] == mine
    scale = jnp.sum(jnp.where(is_mine, every_share, 0.0), axis=1, keepdims=True)
    group_resid = lax.all_gather(resid, "expert", axis=0, tiled=True)
    mixed = lax.psum(partial_value, "expert")
    hidden_in = (group_resid.astype(jnp.float32) + mixed.astype(jnp.float32)).astype(jnp.bfloat16)
    piece = lax.all_gather(hidden_in, "seq", axis=0, tiled=True)
    gate = jnp.dot(piece, w_gate[0], preferred_element_type=jnp.float32)
    upper = jnp.dot(piece, w_up[0], preferred_element_type=jnp.float32)
    hidden = (jax.nn.silu(gate) * upper).astype(jnp.bfloat16)
    part = jnp.dot(hidden, w_down[0], preferred_element_type=jnp.float32)
    part = (part * scale).astype(jnp.bfloat16)
    group_sum = lax.psum_scatter(part, "seq", scatter_dimension=0, tiled=True)
    moe = lax.psum_scatter(group_sum, "expert", scatter_dimension=0, tiled=True)
    own = lax.dynamic_slice_in_dim(hidden_in, mine * rows, rows, 0)
    return (own.astype(jnp.float32) + moe.astype(jnp.float32)).astype(jnp.bfloat16)


def routed_experts(partial_value, resid, w_gate, w_up, w_down, route_ids, route_weight):
    rows = resid.shape[0]
    mixed = lax.psum(partial_value, "expert").astype(jnp.float32)
    own = lax.dynamic_slice_in_dim(mixed, lax.axis_index("expert") * rows, rows, 0)
    hidden_in = (resid.astype(jnp.float32) + own).astype(jnp.bfloat16)
    experts = lax.axis_size("expert")
    capacity = 4 * rows // experts
    flat_ids = route_ids.reshape(-1)
    onehot = (flat_ids[:, None] == jnp.arange(experts, dtype=jnp.int32)[None, :]).astype(jnp.int32)
    rank = jnp.sum(jnp.cumsum(onehot, axis=0) * onehot, axis=1) - 1
    slot = flat_ids * capacity + rank
    placing = (jnp.arange(experts * capacity, dtype=jnp.int32)[:, None] == slot[None, :]).astype(
        jnp.bfloat16
    )
    doubled = jnp.repeat(hidden_in, 2, axis=0)
    outgoing = jnp.dot(placing, doubled, preferred_element_type=jnp.float32).astype(jnp.bfloat16)
    incoming = lax.all_to_all(outgoing, "expert", split_axis=0, concat_axis=0, tiled=True)
    piece = lax.all_gather(incoming, "seq", axis=0, tiled=True)
    gate = jnp.dot(piece, w_gate[0], preferred_element_type=jnp.float32)
    upper = jnp.dot(piece, w_up[0], preferred_element_type=jnp.float32)
    hidden = (jax.nn.silu(gate) * upper).astype(jnp.bfloat16)
    expert_sum = lax.psum_scatter(
        jnp.dot(hidden, w_down[0], preferred_element_type=jnp.float32).astype(jnp.bfloat16),
        "seq",
        scatter_dimension=0,
        tiled=True,
    )
    returned = lax.all_to_all(expert_sum, "expert", split_axis=0, concat_axis=0, tiled=True)
    picked = lax.dot_general(
        placing, returned, (((0,), (0,)), ((), ())), preferred_element_type=jnp.float32
    )
    picked = picked.reshape(rows, 2, -1)
    moe = picked[:, 0] * route_weight[:, 0:1] + picked[:, 1] * route_weight[:, 1:2]
    return (hidden_in.astype(jnp.float32) + moe).astype(jnp.bfloat16)


def local(
    x_in,
    z_in,
    dt_raw,
    bc_in,
    a_log,
    conv_weight,
    conv_bias,
    skip_gain,
    dt_bias,
    out_weight,
    resid,
    w_gate,
    w_up,
    w_down,
    route_ids,
    route_weight,
    grad_mix,
):
    length, channels = x_in.shape
    states = a_log.shape[0]
    rim = KW - 1
    x_val = x_in.astype(jnp.float32)
    z_val = z_in.astype(jnp.float32)
    before = shifted(x_in[length - rim :], "seq", 1)
    padded = jnp.concatenate([before.astype(jnp.float32), x_val], axis=0)
    pre = conv_bias[None, :] + conv_weight[0][None, :] * padded[0:length]
    for tap in range(1, KW):
        pre = pre + conv_weight[tap][None, :] * padded[tap : tap + length]
    conv_sig = jax.nn.sigmoid(pre)
    conv_out = pre * conv_sig
    step = jax.nn.softplus(dt_raw + dt_bias[None, :])
    rate = -jnp.exp(a_log)
    drive = step * conv_out
    z_sig = jax.nn.sigmoid(z_val)
    back_mix = lax.dot_general(
        grad_mix, out_weight, (((1,), (1,)), ((), ())), preferred_element_type=jnp.float32
    )
    grad_y = back_mix * z_val * z_sig

    def grouped(array):
        return array.reshape(length // SUB, SUB, channels)

    def flat(array):
        return array.reshape(length, channels)

    spread = jnp.broadcast_to(
        bc_in.transpose(0, 2, 1)[:, :, :, None], (2, length, states, LANES)
    ).reshape(2, length // SUB, SUB, states, LANES)
    b_wide, c_wide = spread[0], spread[1]
    totals, forward, backward = sweeps(length, channels, states)
    step_g, drive_g, grad_g, conv_g = (grouped(a) for a in (step, drive, grad_y, conv_out))
    own_totals = totals(step_g, drive_g, grad_g, b_wide, c_wide, rate)
    start, arriving = entering(lax.all_gather(own_totals, "seq"))
    y_val = flat(forward(step_g, drive_g, b_wide, c_wide, rate, start))
    y_val = y_val + skip_gain[None, :] * conv_out
    gated = (y_val * z_val * z_sig).astype(jnp.bfloat16)
    partial_value = jnp.dot(gated, out_weight, preferred_element_type=jnp.float32).astype(
        jnp.bfloat16
    )
    experts = dense_experts if lax.axis_size("expert") <= 4 else routed_experts
    layer_out = experts(partial_value, resid, w_gate, w_up, w_down, route_ids, route_weight)
    grad_z = back_mix * y_val * z_sig * (1.0 + z_val * (1.0 - z_sig))
    grad_step, conv_part_grad, grad_b, grad_c, grad_alog_local = backward(
        step_g, drive_g, conv_g, grad_g, b_wide, c_wide, rate, start, arriving
    )
    grad_step, conv_part_grad = flat(grad_step), flat(conv_part_grad)
    grad_conv_out = skip_gain[None, :] * grad_y + conv_part_grad
    grad_skip = jnp.sum(grad_y * conv_out, axis=0)
    grad_dt = grad_step * jax.nn.sigmoid(dt_raw + dt_bias[None, :])
    grad_pre = grad_conv_out * (conv_sig * (1.0 + pre * (1.0 - conv_sig)))
    after = shifted(grad_pre[:rim], "seq", -1)
    grad_pad = jnp.concatenate([grad_pre, after], axis=0)
    grad_x = conv_weight[rim][None, :] * grad_pad[0:length]
    for tap in range(rim):
        grad_x = grad_x + conv_weight[tap][None, :] * grad_pad[rim - tap : rim - tap + length]
    grad_taps = jnp.stack(
        [jnp.sum(grad_pre * padded[tap : tap + length], axis=0) for tap in range(KW)]
    )
    channel_grads = jnp.stack([jnp.sum(grad_pre, axis=0), grad_skip, jnp.sum(grad_dt, axis=0)])
    sums = lax.psum(jnp.concatenate([grad_alog_local, grad_taps, channel_grads], axis=0), "seq")
    grad_alog = sums[:states]
    grad_conv = sums[states : states + KW]
    grad_chan = sums[states + KW :]
    grad_bc = jnp.stack([jnp.sum(grad_b, axis=-1), jnp.sum(grad_c, axis=-1)])
    grad_bc = lax.psum(grad_bc.reshape(2, length, states).transpose(0, 2, 1), "expert")
    return (layer_out, grad_x, grad_z, grad_dt, grad_bc, grad_alog, grad_conv, grad_chan)


def solution(mesh):
    in_specs = (
        P("seq", "expert"),
        P("seq", "expert"),
        P("seq", "expert"),
        P(None, None, "seq"),
        P(None, "expert"),
        P(None, "expert"),
        P("expert"),
        P("expert"),
        P("expert"),
        P("expert", None),
        P(("seq", "expert"), None),
        P("expert", None, "seq"),
        P("expert", None, "seq"),
        P("expert", "seq", None),
        P(("seq", "expert"), None),
        P(("seq", "expert"), None),
        P("seq", None),
    )
    out_specs = (
        P(("seq", "expert"), None),
        P("seq", "expert"),
        P("seq", "expert"),
        P("seq", "expert"),
        P(None, None, "seq"),
        P(None, "expert"),
        P(None, "expert"),
        P(None, "expert"),
    )
    return jax.shard_map(local, mesh=mesh, in_specs=in_specs, out_specs=out_specs, check_vma=False)
```

```python
import jax
import jax.numpy as jnp
from jax import lax
from jax.experimental import pallas as pl
from jax.experimental.pallas import tpu as pltpu
from jax.sharding import PartitionSpec as P

KW = 4
WHOLE_GATHER = False
SUB = 8
LANES = 128


def shifted(x, axis, by):
    peers = lax.axis_size(axis)
    pairs = [(i, i + by) for i in range(peers) if 0 <= i + by < peers]
    return lax.ppermute(x, axis, pairs)


def wide(tile, width):
    return jnp.concatenate([tile] * (width // tile.shape[1]), axis=1)


def folded(value):
    total = value[:, :LANES]
    for at in range(LANES, value.shape[1], LANES):
        total = total + value[:, at : at + LANES]
    return total


def totals_kernel(step_ref, drive_ref, grad_ref, b_ref, c_ref, rate_ref, out_ref):
    rate = rate_ref[...]
    width = rate.shape[1]

    def advance(i, carry):
        state, passed, leaving = carry
        for j in range(SUB):
            decay = jnp.exp(step_ref[i, j : j + 1, :] * rate)
            state = decay * state + drive_ref[i, j : j + 1, :] * wide(b_ref[i, j], width)
            passed = passed * decay
            leaving = leaving + passed * (grad_ref[i, j : j + 1, :] * wide(c_ref[i, j], width))
        return (state, passed, leaving)

    zero = jnp.zeros_like(rate)
    state, passed, leaving = lax.fori_loop(
        0, step_ref.shape[0], advance, (zero, jnp.ones_like(rate), zero)
    )
    out_ref[0] = passed.astype(out_ref.dtype)
    out_ref[1] = state.astype(out_ref.dtype)
    out_ref[2] = leaving.astype(out_ref.dtype)


def forward_kernel(step_ref, drive_ref, b_ref, c_ref, rate_ref, start_ref, y_ref):
    rate = rate_ref[...]
    width = rate.shape[1]

    def advance(i, state):
        for j in range(SUB):
            decay = jnp.exp(step_ref[i, j : j + 1, :] * rate)
            state = decay * state + drive_ref[i, j : j + 1, :] * wide(b_ref[i, j], width)
            y_ref[i, j : j + 1, :] = jnp.sum(
                wide(c_ref[i, j], width) * state, axis=0, keepdims=True
            )
        return state

    lax.fori_loop(0, step_ref.shape[0], advance, start_ref[...])


def backward_kernel(
    step_ref,
    drive_ref,
    conv_ref,
    grad_ref,
    b_ref,
    c_ref,
    rate_ref,
    start_ref,
    arriving_ref,
    step_out_ref,
    conv_out_ref,
    b_out_ref,
    c_out_ref,
    alog_ref,
    states,
):
    rate = rate_ref[...]
    width = rate.shape[1]
    groups = step_ref.shape[0]

    @pl.when(pl.program_id(0) == 0)
    def _():
        b_out_ref[...] = jnp.zeros_like(b_out_ref)
        c_out_ref[...] = jnp.zeros_like(c_out_ref)

    states[0] = start_ref[...]

    def advance(i, state):
        for j in range(SUB):
            decay = jnp.exp(step_ref[i, j : j + 1, :] * rate)
            state = decay * state + drive_ref[i, j : j + 1, :] * wide(b_ref[i, j], width)
            states[i * SUB + j + 1] = state
        return state

    lax.fori_loop(0, groups, advance, start_ref[...])

    def retreat(k, carry):
        flow, alog_sum = carry
        i = groups - 1 - k
        for j in reversed(range(SUB)):
            at = i * SUB + j
            step_now = step_ref[i, j : j + 1, :]
            grad_now = grad_ref[i, j : j + 1, :]
            decay = jnp.exp(step_now * rate)
            adjoint = wide(c_ref[i, j], width) * grad_now + flow
            flow = decay * adjoint
            held = flow * states[at]
            alog_sum = alog_sum + step_now * held
            into_drive = jnp.sum(adjoint * wide(b_ref[i, j], width), axis=0, keepdims=True)
            step_out_ref[i, j : j + 1, :] = (
                jnp.sum(rate * held, axis=0, keepdims=True)
                + conv_ref[i, j : j + 1, :] * into_drive
            )
            conv_out_ref[i, j : j + 1, :] = step_now * into_drive
            b_out_ref[i, j] += folded(adjoint * drive_ref[i, j : j + 1, :])
            c_out_ref[i, j] += folded(grad_now * states[at + 1])
        return (flow, alog_sum)

    _, alog_sum = lax.fori_loop(0, groups, retreat, (arriving_ref[...], jnp.zeros_like(rate)))
    alog_ref[...] = alog_sum * rate


def sweeps(length, channels, states):
    block = min(512, channels)
    groups = length // SUB
    rows = pl.BlockSpec((groups, SUB, block), lambda k: (0, 0, k))
    spread = pl.BlockSpec((groups, SUB, states, LANES), lambda k: (0, 0, 0, 0))
    column = pl.BlockSpec((states, block), lambda k: (0, k))
    grid = (channels // block,)
    f32 = jnp.float32
    row_shape = jax.ShapeDtypeStruct((groups, SUB, channels), f32)
    spread_shape = jax.ShapeDtypeStruct((groups, SUB, states, LANES), f32)
    column_shape = jax.ShapeDtypeStruct((states, channels), f32)
    totals = pl.pallas_call(
        totals_kernel,
        grid=grid,
        in_specs=[rows, rows, rows, spread, spread, column],
        out_specs=pl.BlockSpec((3, states, block), lambda k: (0, 0, k)),
        out_shape=jax.ShapeDtypeStruct((3, states, channels), jnp.bfloat16),
        name="totals",
    )
    forward = pl.pallas_call(
        forward_kernel,
        grid=grid,
        in_specs=[rows, rows, spread, spread, column, column],
        out_specs=rows,
        out_shape=row_shape,
        name="forward",
    )
    backward = pl.pallas_call(
        backward_kernel,
        grid=grid,
        in_specs=[rows, rows, rows, rows, spread, spread, column, column, column],
        out_specs=[rows, rows, spread, spread, column],
        out_shape=[row_shape, row_shape, spread_shape, spread_shape, column_shape],
        scratch_shapes=[pltpu.VMEM((length + 1, states, block), f32)],
        name="backward",
    )
    return totals, forward, backward


def entering(everything):
    peers, here = everything.shape[0], lax.axis_index("seq")
    values = everything.astype(jnp.float32)
    start = jnp.zeros_like(values[0, 0])
    arriving = jnp.zeros_like(start)
    for k in range(peers):
        start = jnp.where(k < here, values[k, 0] * start + values[k, 1], start)
        back = peers - 1 - k
        arriving = jnp.where(back > here, values[back, 0] * arriving + values[back, 2], arriving)
    return start, arriving


def group_shares(route_ids, route_weight, rows):
    experts = lax.axis_size("expert")
    chosen = route_ids[:, :, None] == jnp.arange(experts, dtype=jnp.int32)[None, None, :]
    share = jnp.sum(jnp.where(chosen, route_weight[:, :, None], 0.0), axis=1)
    own = (jnp.arange(experts) == lax.axis_index("expert")).astype(jnp.float32)
    return (own[None, :, None] * share.T[:, None, :]).reshape(experts, experts * rows)


def dense_experts(hidden_in, piece, shares, w_gate, w_up, w_down, rows):
    mine = lax.axis_index("expert")
    gate = jnp.dot(piece, w_gate[0], preferred_element_type=jnp.float32)
    upper = jnp.dot(piece, w_up[0], preferred_element_type=jnp.float32)
    hidden = (jax.nn.silu(gate) * upper).astype(jnp.bfloat16)
    part = jnp.dot(hidden, w_down[0], preferred_element_type=jnp.float32).astype(jnp.bfloat16)
    group_sum = lax.psum_scatter(part, "seq", scatter_dimension=0, tiled=True)
    scale = lax.dynamic_index_in_dim(shares, mine, 0, keepdims=False)[:, None]
    weighted = (group_sum.astype(jnp.float32) * scale).astype(jnp.bfloat16)
    moe = lax.psum_scatter(weighted, "expert", scatter_dimension=0, tiled=True)
    return (hidden_in.astype(jnp.float32) + moe.astype(jnp.float32)).astype(jnp.bfloat16)


def routed_experts(partial_value, resid, w_gate, w_up, w_down, route_ids, route_weight):
    rows = resid.shape[0]
    mixed = lax.psum(partial_value, "expert").astype(jnp.float32)
    own = lax.dynamic_slice_in_dim(mixed, lax.axis_index("expert") * rows, rows, 0)
    hidden_in = (resid.astype(jnp.float32) + own).astype(jnp.bfloat16)
    experts = lax.axis_size("expert")
    capacity = 4 * rows // experts
    flat_ids = route_ids.reshape(-1)
    onehot = (flat_ids[:, None] == jnp.arange(experts, dtype=jnp.int32)[None, :]).astype(jnp.int32)
    rank = jnp.sum(jnp.cumsum(onehot, axis=0) * onehot, axis=1) - 1
    slot = flat_ids * capacity + rank
    placing = (jnp.arange(experts * capacity, dtype=jnp.int32)[:, None] == slot[None, :]).astype(
        jnp.bfloat16
    )
    doubled = jnp.repeat(hidden_in, 2, axis=0)
    outgoing = jnp.dot(placing, doubled, preferred_element_type=jnp.float32).astype(jnp.bfloat16)
    incoming = lax.all_to_all(outgoing, "expert", split_axis=0, concat_axis=0, tiled=True)
    piece = lax.all_gather(incoming, "seq", axis=0, tiled=True)
    gate = jnp.dot(piece, w_gate[0], preferred_element_type=jnp.float32)
    upper = jnp.dot(piece, w_up[0], preferred_element_type=jnp.float32)
    hidden = (jax.nn.silu(gate) * upper).astype(jnp.bfloat16)
    expert_sum = lax.psum_scatter(
        jnp.dot(hidden, w_down[0], preferred_element_type=jnp.float32).astype(jnp.bfloat16),
        "seq",
        scatter_dimension=0,
        tiled=True,
    )
    returned = lax.all_to_all(expert_sum, "expert", split_axis=0, concat_axis=0, tiled=True)
    picked = lax.dot_general(
        placing, returned, (((0,), (0,)), ((), ())), preferred_element_type=jnp.float32
    )
    picked = picked.reshape(rows, 2, -1)
    moe = picked[:, 0] * route_weight[:, 0:1] + picked[:, 1] * route_weight[:, 1:2]
    return (hidden_in.astype(jnp.float32) + moe).astype(jnp.bfloat16)


def local(
    x_in,
    z_in,
    dt_raw,
    bc_in,
    a_log,
    conv_weight,
    conv_bias,
    skip_gain,
    dt_bias,
    out_weight,
    resid,
    w_gate,
    w_up,
    w_down,
    route_ids,
    route_weight,
    grad_mix,
):
    length, channels = x_in.shape
    states = a_log.shape[0]
    rim = KW - 1
    x_val = x_in.astype(jnp.float32)
    z_val = z_in.astype(jnp.float32)
    before = shifted(x_in[length - rim :], "seq", 1)
    padded = jnp.concatenate([before.astype(jnp.float32), x_val], axis=0)
    pre = conv_bias[None, :] + conv_weight[0][None, :] * padded[0:length]
    for tap in range(1, KW):
        pre = pre + conv_weight[tap][None, :] * padded[tap : tap + length]
    conv_sig = jax.nn.sigmoid(pre)
    conv_out = pre * conv_sig
    step = jax.nn.softplus(dt_raw + dt_bias[None, :])
    rate = -jnp.exp(a_log)
    drive = step * conv_out
    z_sig = jax.nn.sigmoid(z_val)
    back_mix = lax.dot_general(
        grad_mix, out_weight, (((1,), (1,)), ((), ())), preferred_element_type=jnp.float32
    )
    grad_y = back_mix * z_val * z_sig

    def grouped(array):
        return array.reshape(length // SUB, SUB, channels)

    def flat(array):
        return array.reshape(length, channels)

    spread = jnp.broadcast_to(
        bc_in.transpose(0, 2, 1)[:, :, :, None], (2, length, states, LANES)
    ).reshape(2, length // SUB, SUB, states, LANES)
    b_wide, c_wide = spread[0], spread[1]
    totals, forward, backward = sweeps(length, channels, states)
    step_g, drive_g, grad_g, conv_g = (grouped(a) for a in (step, drive, grad_y, conv_out))
    own_totals = totals(step_g, drive_g, grad_g, b_wide, c_wide, rate)
    start, arriving = entering(lax.all_gather(own_totals, "seq"))
    y_val = flat(forward(step_g, drive_g, b_wide, c_wide, rate, start))
    y_val = y_val + skip_gain[None, :] * conv_out
    gated = (y_val * z_val * z_sig).astype(jnp.bfloat16)
    partial_value = jnp.dot(gated, out_weight, preferred_element_type=jnp.float32)
    rows = resid.shape[0]
    mine = lax.axis_index("expert")
    experts = lax.axis_size("expert")
    dense = experts <= 4
    if dense:
        own_rows = (jnp.arange(experts) == mine).astype(jnp.float32)[:, None, None]
        placed = (own_rows * resid.astype(jnp.float32)[None]).reshape(partial_value.shape)
        partial_value = (partial_value + placed).astype(jnp.bfloat16)
        if WHOLE_GATHER:
            summed = lax.psum_scatter(partial_value, "expert", scatter_dimension=0, tiled=True)
        else:
            summed = lax.psum(partial_value, "expert")
    grad_z = back_mix * y_val * z_sig * (1.0 + z_val * (1.0 - z_sig))
    grad_step, conv_part_grad, grad_b, grad_c, grad_alog_local = backward(
        step_g, drive_g, conv_g, grad_g, b_wide, c_wide, rate, start, arriving
    )
    grad_step, conv_part_grad = flat(grad_step), flat(conv_part_grad)
    grad_conv_out = skip_gain[None, :] * grad_y + conv_part_grad
    grad_skip = jnp.sum(grad_y * conv_out, axis=0)
    grad_dt = grad_step * jax.nn.sigmoid(dt_raw + dt_bias[None, :])
    grad_pre = grad_conv_out * (conv_sig * (1.0 + pre * (1.0 - conv_sig)))
    after = shifted(grad_pre[:rim], "seq", -1)
    grad_pad = jnp.concatenate([grad_pre, after], axis=0)
    grad_x = conv_weight[rim][None, :] * grad_pad[0:length]
    for tap in range(rim):
        grad_x = grad_x + conv_weight[tap][None, :] * grad_pad[rim - tap : rim - tap + length]
    grad_taps = jnp.stack(
        [jnp.sum(grad_pre * padded[tap : tap + length], axis=0) for tap in range(KW)]
    )
    channel_grads = jnp.stack([jnp.sum(grad_pre, axis=0), grad_skip, jnp.sum(grad_dt, axis=0)])
    own_sums = jnp.concatenate([grad_alog_local, grad_taps, channel_grads], axis=0)
    own_bc = jnp.stack([jnp.sum(grad_b, axis=-1), jnp.sum(grad_c, axis=-1)])
    own_bc = own_bc.reshape(2, length, states).transpose(0, 2, 1).reshape(2 * states, length)
    if dense:
        if WHOLE_GATHER:
            summed, own_sums = lax.optimization_barrier((summed, own_sums))
            hidden_in = summed
            piece = lax.all_gather(hidden_in, ("seq", "expert"), axis=0, tiled=True)
            sums = jnp.sum(lax.all_gather(own_sums, "seq"), axis=0)
        else:
            sums = lax.all_gather(own_sums, "seq")
            summed, sums = lax.optimization_barrier((summed, sums))
            sums = jnp.sum(sums, axis=0)
            hidden_in = lax.dynamic_slice_in_dim(summed, mine * rows, rows, 0)
            piece = lax.all_gather(summed, "seq", axis=0, tiled=True)
        shares = group_shares(route_ids, route_weight, rows)
        joined = lax.psum(jnp.concatenate([own_bc, shares], axis=0), "expert")
        piece, joined, sums = lax.optimization_barrier((piece, joined, sums))
        grad_bc = joined[: 2 * states].reshape(2, states, length)
        layer_out = dense_experts(
            hidden_in, piece, joined[2 * states :], w_gate, w_up, w_down, rows
        )
    else:
        layer_out = routed_experts(
            partial_value.astype(jnp.bfloat16),
            resid,
            w_gate,
            w_up,
            w_down,
            route_ids,
            route_weight,
        )
        sums = lax.psum(own_sums, "seq")
        grad_bc = lax.psum(own_bc, "expert").reshape(2, states, length)
    grad_alog = sums[:states]
    grad_conv = sums[states : states + KW]
    grad_chan = sums[states + KW :]
    return (layer_out, grad_x, grad_z, grad_dt, grad_bc, grad_alog, grad_conv, grad_chan)


def solution(mesh):
    in_specs = (
        P("seq", "expert"),
        P("seq", "expert"),
        P("seq", "expert"),
        P(None, None, "seq"),
        P(None, "expert"),
        P(None, "expert"),
        P("expert"),
        P("expert"),
        P("expert"),
        P("expert", None),
        P(("seq", "expert"), None),
        P("expert", None, "seq"),
        P("expert", None, "seq"),
        P("expert", "seq", None),
        P(("seq", "expert"), None),
        P(("seq", "expert"), None),
        P("seq", None),
    )
    out_specs = (
        P(("seq", "expert"), None),
        P("seq", "expert"),
        P("seq", "expert"),
        P("seq", "expert"),
        P(None, None, "seq"),
        P(None, "expert"),
        P(None, "expert"),
        P(None, "expert"),
    )
    return jax.shard_map(local, mesh=mesh, in_specs=in_specs, out_specs=out_specs, check_vma=False)
```
